256 devices in a mesh: row: 8 (over x_hi, y), col: 32 (over x_lo, z, core).
Axes of the slice: x: 4 (x_hi: 2, x_lo: 2; x = x_hi * 2 + x_lo), y: 4, z: 8, core: 2. Of those that a mesh axis runs over, the one named last changes fastest.
Arguments:
- residuals: bfloat16 [262144, 768], P(('row', 'col')), may hold values from -6 to 6
- codes: int32 [262144, 64], P(('row', 'col')), may hold values from 0 to 255
- list_ids: int32 [262144], P(('row', 'col')), may hold values from 0 to 65535, as said below
- rotation: bfloat16 [768, 768], replicated, may hold values from -0.21875 to 0.21875
- codebook: bfloat16 [256, 768], replicated, may hold values from -6 to 6
- list_fill: int32 [65536], P(('row', 'col')), may hold values from 0 to 4095
Outputs:
- list_drift: float32 [65536, 768], P(('row', 'col'))
- list_counts: int32 [65536], P(('row', 'col'))
- new_blocks: int32 [65536], P(('row', 'col'))
The draws below stay inside these ranges and needn't reach their ends.
Inputs may be any that keep to these rules, and one draw needn't show every extreme that they name: `list_ids`: lists are grouped in blocks of 256 consecutive ids. Among the rows of one device (aligned blocks of 1024 rows), at most 12 have lists in the same block, and in every such aligned block some list block is named by exactly 12 rows.
All inputs are finite; a program needn't handle non-finite values.
Results may differ from the reference program's by a relative error of at most 0.0029.
Values may be sent and summed in bfloat16 or wider, within the bound.
A program may use at most 64 MiB of HBM per device.

```python
import jax
import jax.numpy as jnp
from jax import lax

D = 768
M = 64
KSUB = 256
LISTS_DEV = 256
VEC_DEV = 1024
DSUB = 12
OWNERS = 256
LISTS = 65536
NVEC = 262144
SLOTS = 12


def device_plan(device_key):
    key_hot, key_spread, key_inner, key_order = jax.random.split(device_key, 4)
    hot_owner = jax.random.randint(key_hot, (), 0, OWNERS)
    positions = jax.random.permutation(key_spread, (OWNERS - 1) * SLOTS)[:VEC_DEV - SLOTS]
    others = positions // SLOTS
    others = others + (others >= hot_owner).astype(jnp.int32)
    owner_of = jnp.concatenate([jnp.full((SLOTS,), hot_owner, jnp.int32), others.astype(jnp.int32)])
    inner = jax.random.randint(key_inner, (VEC_DEV,), 0, LISTS_DEV)
    order = jax.random.permutation(key_order, VEC_DEV)
    ids = owner_of * LISTS_DEV + inner
    return ids[order]


def draw_list_ids(key, part):
    base = jax.random.fold_in(key, 7)
    device_keys = jax.vmap(lambda index: jax.random.fold_in(base, index))(jnp.arange(OWNERS))
    return jax.vmap(device_plan)(device_keys).reshape(-1)


def plant(drawn, rng, smallest, high):
    shape = drawn.shape
    index_at = [jax.random.randint(jax.random.fold_in(rng, axis), (), 0, shape[axis]) for axis in range(len(shape))]
    drawn = drawn.at[tuple(index_at)].set(smallest)
    longest = shape.index(max(shape))
    index_at[longest] = (index_at[longest] + 1) % shape[longest]
    return drawn.at[tuple(index_at)].set(high)


def block_levels(stream_key, shape, cuts, low, top_value):
    loudness, own = 1.0, jax.random.fold_in(stream_key, 6)
    for dim, parts in cuts:
        heights = jnp.exp(jax.random.uniform(jax.random.fold_in(own, dim), (parts,), jnp.float32, low / len(cuts), top_value / len(cuts)))
        loudness = loudness * jnp.repeat(heights, shape[dim] // parts).reshape([-1 if axis == dim else 1 for axis in range(len(shape))])
    return loudness


def normal_values(own_key, dims, scale, most, cuts=(), held_as=jnp.bfloat16):
    result = jax.random.normal(own_key, dims, jnp.float32) * scale
    if len(cuts) > 0:
        result = block_levels(own_key, dims, cuts, -0.22, 0.18) * result
    return jnp.clip(result, min=-most, max=most).astype(held_as)


def setup_inputs(seed: int = 0) -> dict:
    splits = jax.random.split(jax.random.key(seed), 7)
    residuals = normal_values(splits[0], (NVEC, D), 1.0, 6.0, ((0, 256),))
    codes = plant(jax.random.randint(splits[1], (NVEC, M), 0, KSUB), jax.random.fold_in(splits[1], 1), 0, KSUB - 1).astype(jnp.int32)
    list_ids = draw_list_ids(jax.random.fold_in(splits[6], 71), 0)
    rotation = normal_values(splits[3], (D, D), D ** -0.5, 0.21875)
    codebook = normal_values(splits[4], (KSUB, D), 1.0, 6.0)
    list_fill = plant(jax.random.randint(splits[5], (LISTS,), 0, 4096), jax.random.fold_in(splits[5], 1), 0, 4095).astype(jnp.int32)
    return {"residuals": residuals, "codes": codes, "list_ids": list_ids, "rotation": rotation, "codebook": codebook, "list_fill": list_fill}


def reference(residuals, codes, list_ids, rotation, codebook, list_fill):
    block_rows = VEC_DEV * 8
    turns = NVEC // block_rows
    code_table = codebook.reshape(KSUB, M, DSUB)
    sub_index = jnp.arange(M, dtype=jnp.int32)

    def step(carry, pieces):
        list_sums, counts = carry
        res_block, code_block, id_block = pieces
        rotated = jnp.dot(res_block, rotation, preferred_element_type=jnp.float32)
        rebuilt = code_table[code_block, sub_index[None, :], :].astype(jnp.float32).reshape(block_rows, D)
        encode_error = (rotated - rebuilt).astype(jnp.bfloat16)
        list_sums = list_sums + jax.ops.segment_sum(encode_error.astype(jnp.float32), id_block, num_segments=LISTS)
        counts = counts + jax.ops.segment_sum(jnp.ones((block_rows,), jnp.int32), id_block, num_segments=LISTS)
        return (list_sums, counts), None

    start = (jnp.zeros((LISTS, D), jnp.float32), jnp.zeros((LISTS,), jnp.int32))
    pieces = (residuals.reshape(turns, block_rows, D), codes.reshape(turns, block_rows, M), list_ids.reshape(turns, block_rows))
    (list_sums, list_counts), _ = lax.scan(step, start, pieces)
    divisor = jnp.maximum(list_counts, 1).astype(jnp.float32)
    list_drift = list_sums / divisor[:, None]
    new_blocks = (list_fill + list_counts + 127) // 128 - (list_fill + 127) // 128
    return list_drift, list_counts, new_blocks
```

```python
import functools

import jax
import jax.numpy as jnp
from jax import lax
from jax.experimental import pallas as pl
from jax.experimental.pallas import tpu as pltpu
from jax.sharding import PartitionSpec as P

MESH = pl.DeviceIdType.MESH
D = 768
M = 64
DSUB = 12
KSUB = 256
VEC = 1024
LISTS = 256
PEERS = 32
ZS = 8
F32 = jnp.float32
BF = jnp.bfloat16

_RING = (
    [(1, 2), (2, 1), (3, 2), (2, 3), (2, 2)]
    + [(1, 1), (3, 3), (1, 3), (3, 1)]
    + [(2, 0), (0, 2)]
    + [(1, 0), (0, 1), (3, 0), (0, 3)]
)
ORDER = [(a, b, 0) for a, b in _RING] + [(a, b, 1) for a, b in _RING] + [(0, 0, 1)]


def coords():
    row = lax.axis_index("row")
    col = lax.axis_index("col")
    return (row // 4) * 2 + col // 16, row % 4, (col // 2) % 8, col % 2


def device(x, y, z, c):
    return ((x // 2) * 4 + y, (x % 2) * 16 + z * 2 + c)


def encode_kernel(cap, group, chunks, me_ref, res_ref, codes_ref, ids_ref, rot_ref, book_ref,
                  slots_ref, tags_ref, table_ref, built_ref, err_ref):
    width = D // chunks
    lanes = cap * group
    ids = ids_ref[...]
    owner = ids // LISTS
    inner = ids % LISTS
    col = owner % 32
    row = owner // 32
    zed = (col // 2) % 8
    spot = (((row // 4) * 2 + col // 16) * 4 + row % 4) * 2 + col % 2
    at_peer = (lax.broadcasted_iota(jnp.int32, (PEERS, VEC), 0) == spot).astype(F32)

    blocks = jnp.concatenate([at_peer[:, b * 128:(b + 1) * 128] for b in range(VEC // 128)], axis=0).astype(BF)
    before = (lax.broadcasted_iota(jnp.int32, (128, 128), 0) < lax.broadcasted_iota(jnp.int32, (128, 128), 1)).astype(BF)
    inside = jnp.dot(blocks, before, preferred_element_type=F32)
    whole = jnp.dot(blocks, jnp.ones((128, 128), BF), preferred_element_type=F32)
    offset = jnp.zeros((PEERS, 128), F32)
    ranks = []
    for b in range(VEC // 128):
        part = inside[b * PEERS:(b + 1) * PEERS] + offset
        ranks.append(jnp.sum(part * at_peer[:, b * 128:(b + 1) * 128], axis=0, keepdims=True))
        offset = offset + whole[b * PEERS:(b + 1) * PEERS]
    rank = jnp.concatenate(ranks, axis=1).astype(jnp.int32)
    slot = spot * cap + rank

    lane = rank + cap * (me_ref[0] % group)
    lane_hot = (lax.broadcasted_iota(jnp.int32, (lanes, VEC), 0) == lane).astype(F32).astype(BF)
    tag_rows = jnp.concatenate([at_peer * (zed + 1).astype(F32), at_peer * inner.astype(F32)], axis=0).astype(BF)
    found = lax.dot_general(tag_rows, lane_hot, (((1,), (1,)), ((), ())), preferred_element_type=F32)
    tags = (found[:PEERS] - 1.0) * LISTS + found[PEERS:]
    tags_ref[...] = tags.astype(jnp.int32).reshape(PEERS, 1, lanes)

    line = lax.broadcasted_iota(jnp.int32, (D, D), 0)
    feature = (line % M) * DSUB + line // M
    perm = (lax.broadcasted_iota(jnp.int32, (D, D), 1) == feature).astype(F32).astype(BF)
    table_ref[...] = lax.dot_general(perm, book_ref[...], (((1,), (1,)), ((), ())), preferred_element_type=F32)
    codes = codes_ref[...]
    for j in range(DSUB):
        low = table_ref[j * M:(j + 1) * M, :128]
        high = table_ref[j * M:(j + 1) * M, 128:]
        for b in range(VEC // 128):
            index = codes[:, b * 128:(b + 1) * 128]
            near = index % 128
            picked = jnp.where(
                index < 128,
                jnp.take_along_axis(low, near, axis=1, mode="promise_in_bounds"),
                jnp.take_along_axis(high, near, axis=1, mode="promise_in_bounds"),
            )
            built_ref[j * M:(j + 1) * M, b * 128:(b + 1) * 128] = picked.astype(BF)
    rebuilt = lax.dot_general(built_ref[...], perm, (((0,), (0,)), ((), ())), preferred_element_type=F32)
    rotated = jnp.dot(res_ref[...], rot_ref[...], preferred_element_type=F32)
    err_ref[...] = (rotated - rebuilt).astype(BF)

    rows = 256

    def place(i, _):
        start = pl.multiple_of(i * rows, rows)
        pick = (lax.broadcasted_iota(jnp.int32, (rows, VEC), 0) + start == slot).astype(F32).astype(BF)
        for k in range(chunks):
            moved = jnp.dot(pick, err_ref[:, k * width:(k + 1) * width], preferred_element_type=F32)
            slots_ref[k, pl.ds(start, rows), :] = moved.astype(BF)
        return 0

    lax.fori_loop(0, PEERS * cap // rows, place, 0)


def encode(cap, group, chunks, me, residuals, codes, ids, rotation, codebook):
    vmem = pl.BlockSpec(memory_space=pltpu.VMEM)
    return pl.pallas_call(
        functools.partial(encode_kernel, cap, group, chunks),
        out_shape=(
            jax.ShapeDtypeStruct((chunks, PEERS * cap, D // chunks), BF),
            jax.ShapeDtypeStruct((PEERS, 1, cap * group), jnp.int32),
        ),
        in_specs=[pl.BlockSpec(memory_space=pltpu.SMEM)] + [vmem] * 5,
        out_specs=(vmem, vmem),
        scratch_shapes=[
            pltpu.VMEM((D, KSUB), F32),
            pltpu.VMEM((D, VEC), BF),
            pltpu.VMEM((VEC, D), BF),
        ],
        compiler_params=pltpu.CompilerParams(vmem_limit_bytes=50 * 2**20),
    )(me, residuals, codes, ids, rotation, codebook)


def exchange_kernel(cap, group, chunks, slots_ref, tags_ref, sums_ref, counts_ref,
                    rows, tag_in, hot, part, z_out, z_in, cnt_out, cnt_in,
                    row_ssem, row_rsem, own_sem, tag_ssem, tag_rsem, tag_own,
                    z_ssem, z_rsem, cnt_ssem, cnt_rsem):
    x, y, z, c = coords()
    me = (x * 4 + y) * 2 + c
    width = D // chunks
    half = width // 2
    lanes = cap * group

    barrier = pltpu.get_barrier_semaphore()
    for dx, dy, dc in ORDER:
        pl.semaphore_signal(barrier, inc=1, device_id=device((x + dx) % 4, (y + dy) % 4, z, (c + dc) % 2), device_id_type=MESH)
    for dz in range(1, ZS):
        pl.semaphore_signal(barrier, inc=1, device_id=device(x, y, (z + dz) % 8, c), device_id_type=MESH)
    pl.semaphore_wait(barrier, len(ORDER) + ZS - 1)

    def peer(o):
        dx, dy, dc = o
        px, py, pc = (x + dx) % 4, (y + dy) % 4, (c + dc) % 2
        return (px * 4 + py) * 2 + pc, device(px, py, z, pc)

    def tag_copy(k):
        spot, dev = peer(ORDER[k])
        return pltpu.make_async_remote_copy(
            tags_ref.at[spot], tag_in.at[me], tag_ssem.at[k], tag_rsem.at[k], device_id=dev, device_id_type=MESH)

    def row_copy(ch, k):
        spot, dev = peer(ORDER[k])
        return pltpu.make_async_remote_copy(
            slots_ref.at[ch, pl.ds(pl.multiple_of(spot * cap, 16), cap)],
            rows.at[ch, pl.ds(pl.multiple_of(me * cap, 16), cap)],
            row_ssem.at[ch, k], row_rsem.at[ch, k], device_id=dev, device_id_type=MESH)

    def own_copy(ch):
        span = pl.ds(pl.multiple_of(me * cap, 16), cap)
        return pltpu.make_async_copy(slots_ref.at[ch, span], rows.at[ch, span], own_sem.at[ch])

    def tag_keep():
        return pltpu.make_async_copy(tags_ref.at[me], tag_in.at[me], tag_own)

    for k in range(len(ORDER)):
        tag_copy(k).start()
    tag_keep().start()

    def start_rows(ch, _):
        for k in range(len(ORDER)):
            row_copy(ch, k).start()
        own_copy(ch).start()
        return 0

    lax.fori_loop(0, chunks, start_rows, 0)

    for k in range(len(ORDER)):
        tag_copy(k).wait()
    tag_keep().wait()

    eye = (lax.broadcasted_iota(jnp.int32, (128, 128), 0) == lax.broadcasted_iota(jnp.int32, (128, 128), 1)).astype(F32)

    def make_hot(d, _):
        names = lax.broadcasted_iota(jnp.int32, (LISTS, 128), 0) + d * LISTS
        total = jnp.zeros((LISTS, 128), F32)
        for q in range(PEERS // group):
            tag = tag_in[q * group]
            for i in range(1, group):
                tag = jnp.maximum(tag, tag_in[q * group + i])
            for j in range(lanes // 128):
                one = (names == tag[:, j * 128:(j + 1) * 128]).astype(F32)
                total = total + one
                hot[d, :, q * lanes + j * 128:q * lanes + (j + 1) * 128] = one.astype(BF)
        spread = jnp.dot(total.astype(BF), jnp.ones((128, 128), BF), preferred_element_type=F32)
        for b in range(LISTS // 128):
            cnt_out[d, :, b * 128:(b + 1) * 128] = jnp.sum(spread[b * 128:(b + 1) * 128] * eye, axis=0, keepdims=True)
        return 0

    lax.fori_loop(0, ZS, make_hot, 0)

    def cnt_copy(dz):
        to = (z + dz) % 8
        return pltpu.make_async_remote_copy(
            cnt_out.at[to], cnt_in.at[z], cnt_ssem.at[dz], cnt_rsem.at[dz],
            device_id=device(x, y, to, c), device_id_type=MESH)

    for dz in range(1, ZS):
        cnt_copy(dz).start()

    def length(h, s):
        return 4 if h == s else 3

    def z_copy(ch, h, s, t):
        to = (z + (1 if s == 0 else 7)) % 8
        return pltpu.make_async_remote_copy(
            z_out.at[ch, h, s, t], z_in.at[ch, h, s, t], z_ssem.at[ch, h, s, t], z_rsem.at[ch, h, s, t],
            device_id=device(x, y, to, c), device_id_type=MESH)

    def finish(ch, _):
        for k in range(len(ORDER)):
            row_copy(ch, k).wait()
        own_copy(ch).wait()

        def table(d):
            return jnp.dot(hot[d], rows[ch], preferred_element_type=F32)

        far = table((z + 4) % 8)
        for h in (0, 1):
            z_out[ch, h, h, 0] = far[:, h * half:(h + 1) * half].astype(BF)
            z_copy(ch, h, h, 0).start()
        for s in (0, 1):
            near = table((z + (3 if s == 0 else 5)) % 8)
            part[3, s] = near
            h = 1 - s
            z_out[ch, h, s, 0] = near[:, h * half:(h + 1) * half].astype(BF)
            z_copy(ch, h, s, 0).start()
        for k in (2, 1):
            for s in (0, 1):
                part[k, s] = table((z + (k if s == 0 else 8 - k)) % 8)
        part[0, 0] = table(z)
        for k in (3, 2, 1):
            for s in (0, 1):
                for h in (0, 1):
                    t = length(h, s) - k
                    if t > 0:
                        z_copy(ch, h, s, t - 1).wait_recv()
                        own = part[k, s, :, h * half:(h + 1) * half]
                        z_out[ch, h, s, t] = (own + z_in[ch, h, s, t - 1].astype(F32)).astype(BF)
                        z_copy(ch, h, s, t).start()
        for h in (0, 1):
            total = part[0, 0, :, h * half:(h + 1) * half]
            for s in (0, 1):
                last = length(h, s) - 1
                z_copy(ch, h, s, last).wait_recv()
                total = total + z_in[ch, h, s, last].astype(F32)
            sums_ref[ch, h] = total
        return 0

    lax.fori_loop(0, chunks, finish, 0)

    def drain(ch, _):
        for h in (0, 1):
            for s in (0, 1):
                for t in range(length(h, s)):
                    z_copy(ch, h, s, t).wait_send()
        return 0

    lax.fori_loop(0, chunks, drain, 0)

    total = cnt_out[z]
    for dz in range(1, ZS):
        cnt_copy(dz).wait()
        total = total + cnt_in[(z + 8 - dz) % 8]
    counts_ref[...] = total


def exchange(cap, group, chunks, slots, tags):
    vmem = pl.BlockSpec(memory_space=pltpu.VMEM)
    width = D // chunks
    half = width // 2
    n = len(ORDER)
    lanes = cap * group
    dma = pltpu.SemaphoreType.DMA
    return pl.pallas_call(
        functools.partial(exchange_kernel, cap, group, chunks),
        out_shape=(
            jax.ShapeDtypeStruct((chunks, 2, LISTS, half), F32),
            jax.ShapeDtypeStruct((1, LISTS), F32),
        ),
        in_specs=[pl.BlockSpec(memory_space=pl.ANY), vmem],
        out_specs=(vmem, vmem),
        scratch_shapes=[
            pltpu.VMEM((chunks, PEERS * cap, width), BF),
            pltpu.VMEM((PEERS, 1, lanes), jnp.int32),
            pltpu.VMEM((ZS, LISTS, PEERS * cap), BF),
            pltpu.VMEM((4, 2, LISTS, width), F32),
            pltpu.VMEM((chunks, 2, 2, 4, LISTS, half), BF),
            pltpu.VMEM((chunks, 2, 2, 4, LISTS, half), BF),
            pltpu.VMEM((ZS, 1, LISTS), F32),
            pltpu.VMEM((ZS, 1, LISTS), F32),
            dma((chunks, n)), dma((chunks, n)), dma((chunks,)),
            dma((n,)), dma((n,)), dma,
            dma((chunks, 2, 2, 4)), dma((chunks, 2, 2, 4)),
            dma((ZS,)), dma((ZS,)),
        ],
        compiler_params=pltpu.CompilerParams(
            collective_id=0, has_side_effects=True, vmem_limit_bytes=60 * 2**20),
    )(slots, tags)


def local(residuals, codes, list_ids, rotation, codebook, list_fill):
    x, y, z, c = coords()
    me = ((x * 4 + y) * 2 + c).reshape(1)
    cap, group, chunks = 96, 4, 3
    slots, tags = encode(cap, group, chunks, me, residuals, codes.T, list_ids.reshape(1, VEC), rotation, codebook)
    sums, counts = exchange(cap, group, chunks, slots, tags)
    list_counts = counts.reshape(LISTS).astype(jnp.int32)
    divisor = jnp.maximum(list_counts, 1).astype(F32)
    sums = jnp.transpose(sums.reshape(chunks * 2, LISTS, D // chunks // 2), (1, 0, 2)).reshape(LISTS, D)
    list_drift = sums / divisor[:, None]
    new_blocks = (list_fill + list_counts + 127) // 128 - (list_fill + 127) // 128
    return list_drift, list_counts, new_blocks


def solution(mesh):
    split = P(("row", "col"))
    wide = P(("row", "col"), None)
    return jax.shard_map(
        local,
        mesh=mesh,
        in_specs=(wide, wide, split, P(), P(), split),
        out_specs=(wide, split, split),
        check_vma=False,
    )
```

```python
import functools

import jax
import jax.numpy as jnp
from jax import lax
from jax.experimental import pallas as pl
from jax.experimental.pallas import tpu as pltpu
from jax.sharding import PartitionSpec as P

MESH = pl.DeviceIdType.MESH
D = 768
M = 64
DSUB = 12
KSUB = 256
VEC = 1024
LISTS = 256
PEERS = 32
ZS = 8
CHUNKS = 6
WIDTH = D // CHUNKS
HALF = LISTS // 2
F32 = jnp.float32
BF = jnp.bfloat16

_RING = (
    [(1, 2), (2, 1), (3, 2), (2, 3), (2, 2)]
    + [(1, 1), (3, 3), (1, 3), (3, 1)]
    + [(2, 0), (0, 2)]
    + [(1, 0), (0, 1), (3, 0), (0, 3)]
)
ORDER = [(a, b, 0) for a, b in _RING] + [(a, b, 1) for a, b in _RING] + [(0, 0, 1)]


def coords():
    row = lax.axis_index("row")
    col = lax.axis_index("col")
    return (row // 4) * 2 + col // 16, row % 4, (col // 2) % 8, col % 2


def device(x, y, z, c):
    return ((x // 2) * 4 + y, (x % 2) * 16 + z * 2 + c)


def greet(barrier, x, y, z, c):
    for dx, dy, dc in ORDER:
        pl.semaphore_signal(barrier, inc=1, device_id=device((x + dx) % 4, (y + dy) % 4, z, (c + dc) % 2), device_id_type=MESH)
    for dz in range(1, ZS):
        pl.semaphore_signal(barrier, inc=1, device_id=device(x, y, (z + dz) % 8, c), device_id_type=MESH)


def one_hot(names, index, start, size):
    shifted = index - start
    inside = jnp.logical_and(shifted >= 0, shifted < size)
    row = jnp.where(inside, shifted, -1).astype(F32).astype(BF)
    return jnp.where(names == row, jnp.ones((), BF), jnp.zeros((), BF))


def encode_kernel(res_hbm, codes_hbm, ids_ref, rot_hbm, book_hbm, err_ref, plan_ref, most_ref,
                  res_ref, codes_ref, rot_ref, book_ref, table_ref, built_ref,
                  here_out, here_in, all_out, all_in, sems, here_ssem, here_rsem, all_ssem, all_rsem):
    x, y, z, c = coords()
    barrier = pltpu.get_barrier_semaphore()
    greet(barrier, x, y, z, c)
    loads = [
        pltpu.make_async_copy(src, dst, sems.at[i])
        for i, (src, dst) in enumerate(
            [(book_hbm, book_ref), (codes_hbm, codes_ref), (res_hbm, res_ref), (rot_hbm, rot_ref)])
    ]
    for load in loads:
        load.start()

    ids = ids_ref[...]
    owner = ids // LISTS
    inner = ids % LISTS
    col = owner % 32
    row = owner // 32
    zed = (col // 2) % 8
    spot = (((row // 4) * 2 + col // 16) * 4 + row % 4) * 2 + col % 2
    at_peer = (lax.broadcasted_iota(jnp.int32, (PEERS, VEC), 0) == spot).astype(F32)
    blocks = jnp.concatenate([at_peer[:, b * 128:(b + 1) * 128] for b in range(VEC // 128)], axis=0).astype(BF)
    before = (lax.broadcasted_iota(jnp.int32, (128, 128), 0) < lax.broadcasted_iota(jnp.int32, (128, 128), 1)).astype(F32).astype(BF)
    inside = jnp.dot(blocks, before, preferred_element_type=F32)
    whole = jnp.dot(blocks, jnp.ones((128, 128), BF), preferred_element_type=F32)
    offset = jnp.zeros((PEERS, 128), F32)
    for b in range(VEC // 128):
        part = inside[b * PEERS:(b + 1) * PEERS] + offset
        rank = jnp.sum(part * at_peer[:, b * 128:(b + 1) * 128], axis=0, keepdims=True)
        plan_ref[1:2, b * 128:(b + 1) * 128] = rank.astype(jnp.int32)
        offset = offset + whole[b * PEERS:(b + 1) * PEERS]
    here_out[...] = jnp.max(offset, axis=0, keepdims=True)
    pl.semaphore_wait(barrier, len(ORDER) + ZS - 1)
    for k, (dx, dy, dc) in enumerate(ORDER):
        pltpu.make_async_remote_copy(
            here_out, here_in.at[k], here_ssem, here_rsem,
            device_id=device((x + dx) % 4, (y + dy) % 4, z, (c + dc) % 2), device_id_type=MESH).start()
    plan_ref[0:1, :] = spot
    plan_ref[2:3, :] = zed
    plan_ref[3:4, :] = inner
    plan_ref[4:8, :] = jnp.zeros((4, VEC), jnp.int32)

    line = lax.broadcasted_iota(jnp.int32, (D, D), 0)
    feature = (line % M) * DSUB + line // M
    perm = (lax.broadcasted_iota(jnp.int32, (D, D), 1) == feature).astype(F32).astype(BF)
    for load in loads:
        load.wait()
    table_ref[...] = lax.dot_general(perm, book_ref[...], (((1,), (1,)), ((), ())), preferred_element_type=F32)
    codes = codes_ref[...]
    for j in range(DSUB):
        low = table_ref[j * M:(j + 1) * M, :128]
        high = table_ref[j * M:(j + 1) * M, 128:]
        for b in range(VEC // 128):
            index = codes[:, b * 128:(b + 1) * 128]
            near = index % 128
            picked = jnp.where(
                index < 128,
                jnp.take_along_axis(low, near, axis=1, mode="promise_in_bounds"),
                jnp.take_along_axis(high, near, axis=1, mode="promise_in_bounds"),
            )
            built_ref[j * M:(j + 1) * M, b * 128:(b + 1) * 128] = picked.astype(BF)
    pltpu.make_async_copy(here_in, here_in, here_rsem).wait()
    most = here_out[...]
    for k in range(len(ORDER)):
        most = jnp.maximum(most, here_in[k])
    all_out[...] = most
    for dz in range(1, ZS):
        pltpu.make_async_remote_copy(
            all_out, all_in.at[dz - 1], all_ssem, all_rsem,
            device_id=device(x, y, (z + dz) % 8, c), device_id_type=MESH).start()
    rebuilt = lax.dot_general(built_ref[...], perm, (((0,), (0,)), ((), ())), preferred_element_type=F32)
    rotated = jnp.dot(res_ref[...], rot_ref[...], preferred_element_type=F32)
    error = (rotated - rebuilt).astype(BF)
    for k in range(CHUNKS):
        err_ref[k] = error[:, k * WIDTH:(k + 1) * WIDTH]
    pltpu.make_async_copy(all_in, all_in, all_rsem).wait()
    for i in range(ZS - 1):
        most = jnp.maximum(most, all_in[i])
    most_ref[...] = most.astype(jnp.int32)
    pltpu.make_async_copy(here_in, here_in, here_ssem).wait()
    pltpu.make_async_copy(all_in, all_in, all_ssem).wait()


def encode(residuals, codes, ids, rotation, codebook):
    vmem = pl.BlockSpec(memory_space=pltpu.VMEM)
    hbm = pl.BlockSpec(memory_space=pltpu.HBM)
    return pl.pallas_call(
        encode_kernel,
        out_shape=(
            jax.ShapeDtypeStruct((CHUNKS, VEC, WIDTH), BF),
            jax.ShapeDtypeStruct((8, VEC), jnp.int32),
            jax.ShapeDtypeStruct((1, 128), jnp.int32),
        ),
        in_specs=[hbm, hbm, vmem, hbm, hbm],
        out_specs=(vmem, vmem, vmem),
        scratch_shapes=[
            pltpu.VMEM((VEC, D), BF),
            pltpu.VMEM((M, VEC), jnp.int32),
            pltpu.VMEM((D, D), BF),
            pltpu.VMEM((KSUB, D), BF),
            pltpu.VMEM((D, KSUB), F32),
            pltpu.VMEM((D, VEC), BF),
            pltpu.VMEM((1, 128), F32),
            pltpu.VMEM((PEERS - 1, 1, 128), F32),
            pltpu.VMEM((1, 128), F32),
            pltpu.VMEM((ZS - 1, 1, 128), F32),
            pltpu.SemaphoreType.DMA((4,)),
            pltpu.SemaphoreType.DMA, pltpu.SemaphoreType.DMA,
            pltpu.SemaphoreType.DMA, pltpu.SemaphoreType.DMA,
        ],
        compiler_params=pltpu.CompilerParams(
            collective_id=0, has_side_effects=True, vmem_limit_bytes=63 * 2**20),
    )(residuals, codes, ids, rotation, codebook)


def exchange_kernel(cap, group, err_ref, plan_ref, sums_ref, counts_ref,
                    pick, slots, rows, tag_out, tag_in, hot, part, z_out, z_in, cnt_out, cnt_in,
                    row_ssem, row_rsem, tag_ssem, tag_rsem,
                    z_ssem, z_rsem, cnt_ssem, cnt_rsem):
    x, y, z, c = coords()
    me = (x * 4 + y) * 2 + c
    lanes = cap * group
    total_slots = PEERS * cap

    barrier = pltpu.get_barrier_semaphore()
    greet(barrier, x, y, z, c)

    def peer(o):
        dx, dy, dc = o
        px, py, pc = (x + dx) % 4, (y + dy) % 4, (c + dc) % 2
        return (px * 4 + py) * 2 + pc, device(px, py, z, pc)

    def tag_copy(k):
        spot, dev = peer(ORDER[k])
        return pltpu.make_async_remote_copy(
            tag_out.at[spot], tag_in.at[me], tag_ssem, tag_rsem, device_id=dev, device_id_type=MESH)

    def row_copy(ch, k):
        spot, dev = peer(ORDER[k])
        return pltpu.make_async_remote_copy(
            slots.at[ch, pl.ds(pl.multiple_of(spot * cap, 16), cap)],
            rows.at[ch, pl.ds(pl.multiple_of(me * cap, 16), cap)],
            row_ssem.at[ch], row_rsem.at[ch], device_id=dev, device_id_type=MESH)

    def own_copy(ch):
        span = pl.ds(pl.multiple_of(me * cap, 16), cap)
        return pltpu.make_async_copy(slots.at[ch, span], rows.at[ch, span], row_rsem.at[ch])

    def tag_keep():
        return pltpu.make_async_copy(tag_out.at[me], tag_in.at[me], tag_rsem)

    spot = plan_ref[0:1, :]
    rank = plan_ref[1:2, :]
    at_peer = (lax.broadcasted_iota(jnp.int32, (PEERS, VEC), 0) == spot).astype(F32)
    lane = rank + cap * (me % group)
    wide_names = lax.broadcasted_iota(jnp.int32, (LISTS, VEC), 0).astype(F32).astype(BF)
    lane_hot = jnp.concatenate([one_hot(wide_names[:128], lane, j * 128, 128) for j in range(lanes // 128)], axis=0)
    tag_rows = jnp.concatenate(
        [at_peer * (plan_ref[2:3, :] + 1).astype(F32), at_peer * plan_ref[3:4, :].astype(F32)], axis=0).astype(BF)
    found = lax.dot_general(tag_rows, lane_hot, (((1,), (1,)), ((), ())), preferred_element_type=F32)
    tags = (found[:PEERS] - 1.0) * LISTS + found[PEERS:]
    tag_out[...] = tags.astype(jnp.int32).reshape(PEERS, 1, lanes)

    slot = spot * cap + rank

    def place_first(i, _):
        start = pl.multiple_of(i * 256, 256)
        one = one_hot(wide_names, slot, start, 256)
        pick[pl.ds(start, 256), :] = one
        slots[0, pl.ds(start, 256), :] = jnp.dot(one, err_ref[0], preferred_element_type=F32).astype(BF)
        return 0

    def place(ch):
        def one(i, _):
            start = pl.multiple_of(i * 512, 512)
            slots[ch, pl.ds(start, 512), :] = jnp.dot(
                pick[pl.ds(start, 512), :], err_ref[ch], preferred_element_type=F32).astype(BF)
            return 0

        lax.fori_loop(0, total_slots // 512, one, 0)

    def send(ch):
        for k in range(len(ORDER)):
            row_copy(ch, k).start()
        own_copy(ch).start()

    lax.fori_loop(0, total_slots // 256, place_first, 0)
    pl.semaphore_wait(barrier, len(ORDER) + ZS - 1)
    for k in range(len(ORDER)):
        tag_copy(k).start()
    tag_keep().start()
    send(0)
    place(1)
    send(1)

    pltpu.make_async_copy(tag_in, tag_in, tag_rsem).wait()
    others = pl.ds(0, PEERS - 1)
    pltpu.make_async_copy(tag_out.at[others], tag_out.at[others], tag_ssem).wait()

    eye = (lax.broadcasted_iota(jnp.int32, (128, 128), 0) == lax.broadcasted_iota(jnp.int32, (128, 128), 1)).astype(F32)

    names = lax.broadcasted_iota(jnp.int32, (LISTS, 128), 0).astype(F32).astype(BF)
    tag = []
    for q in range(PEERS // group):
        joined = tag_in[q * group]
        for i in range(1, group):
            joined = jnp.maximum(joined, tag_in[q * group + i])
        tag += [joined[:, j * 128:(j + 1) * 128] for j in range(lanes // 128)]

    def make_hot(d, _):
        total = jnp.zeros((LISTS, 128), BF)
        for j in range(total_slots // 128):
            one = one_hot(names, tag[j], d * LISTS, LISTS)
            total = total + one
            hot[d, :, j * 128:(j + 1) * 128] = one
        spread = jnp.dot(total, jnp.ones((128, 128), BF), preferred_element_type=F32)
        for b in range(LISTS // 128):
            cnt_out[d, :, b * 128:(b + 1) * 128] = jnp.sum(spread[b * 128:(b + 1) * 128] * eye, axis=0, keepdims=True)
        return 0

    lax.fori_loop(0, ZS, make_hot, 0)

    def cnt_copy(dz):
        to = (z + dz) % 8
        return pltpu.make_async_remote_copy(
            cnt_out.at[to], cnt_in.at[z], cnt_ssem.at[dz], cnt_rsem.at[dz],
            device_id=device(x, y, to, c), device_id_type=MESH)

    for dz in range(1, ZS):
        cnt_copy(dz).start()

    def length(h, s):
        return 4 if h == s else 3

    def z_copy(ch, h, s, t):
        to = (z + (1 if s == 0 else 7)) % 8
        return pltpu.make_async_remote_copy(
            z_out.at[ch, h, s, t], z_in.at[ch, h, s, t], z_ssem.at[ch], z_rsem.at[ch, h, s, t],
            device_id=device(x, y, to, c), device_id_type=MESH)

    def table(ch, d):
        return jnp.dot(hot[d], rows[ch], preferred_element_type=F32)

    def reduce(ch):
        pltpu.make_async_copy(rows.at[ch], rows.at[ch], row_rsem.at[ch]).wait()
        flip = ch % 2
        far = table(ch, (z + 4) % 8)
        for h in (0, 1):
            z_out[ch, h, h, 0] = far[h * HALF:(h + 1) * HALF].astype(BF)
            z_copy(ch, h, h, 0).start()
        for s in (0, 1):
            near = table(ch, (z + (3 if s == 0 else 5)) % 8)
            part[flip, 3, s] = near
            h = 1 - s
            z_out[ch, h, s, 0] = near[h * HALF:(h + 1) * HALF].astype(BF)
            z_copy(ch, h, s, 0).start()
        for k in (2, 1):
            for s in (0, 1):
                part[flip, k, s] = table(ch, (z + (k if s == 0 else 8 - k)) % 8)
        part[flip, 0, 0] = table(ch, z)

    def hop(ch, k):
        flip = ch % 2
        for h in (0, 1):
            for s in (0, 1):
                t = length(h, s) - k
                if t > 0:
                    z_copy(ch, h, s, t - 1).wait_recv()
                    own = part[flip, k, s, h * HALF:(h + 1) * HALF]
                    z_out[ch, h, s, t] = (own + z_in[ch, h, s, t - 1].astype(F32)).astype(BF)
                    z_copy(ch, h, s, t).start()

    def settle(ch):
        flip = ch % 2
        for h in (0, 1):
            total = part[flip, 0, 0, h * HALF:(h + 1) * HALF]
            for s in (0, 1):
                last = length(h, s) - 1
                z_copy(ch, h, s, last).wait_recv()
                total = total + z_in[ch, h, s, last].astype(F32)
            sums_ref[h * HALF:(h + 1) * HALF, pl.ds(pl.multiple_of(ch * WIDTH, WIDTH), WIDTH)] = total

    def round_trip(ch, _):
        reduce(ch)

        @pl.when(ch > 0)
        def _():
            hop(ch - 1, 1)

        hop(ch, 3)

        @pl.when(ch + 2 < CHUNKS)
        def _():
            place(ch + 2)
            send(ch + 2)

        @pl.when(ch > 0)
        def _():
            settle(ch - 1)

        hop(ch, 2)
        return 0

    lax.fori_loop(0, CHUNKS, round_trip, 0)
    hop(CHUNKS - 1, 1)
    settle(CHUNKS - 1)

    def drain(ch, _):
        others = slots.at[ch, pl.ds(0, (PEERS - 1) * cap)]
        pltpu.make_async_copy(others, others, row_ssem.at[ch]).wait()
        first = z_out.at[ch, 0]
        rest = z_out.at[ch, 1, pl.ds(0, 1)]
        pltpu.make_async_copy(first, first, z_ssem.at[ch]).wait()
        pltpu.make_async_copy(rest, rest, z_ssem.at[ch]).wait()
        tip = z_out.at[ch, 1, 1, pl.ds(0, 2)]
        pltpu.make_async_copy(tip, tip, z_ssem.at[ch]).wait()
        return 0

    lax.fori_loop(0, CHUNKS, drain, 0)

    total = cnt_out[z]
    for dz in range(1, ZS):
        cnt_copy(dz).wait()
        total = total + cnt_in[(z + 8 - dz) % 8]
    counts_ref[...] = total


def exchange(cap, group, number, err, plan):
    vmem = pl.BlockSpec(memory_space=pltpu.VMEM)
    lanes = cap * group
    dma = pltpu.SemaphoreType.DMA
    return pl.pallas_call(
        functools.partial(exchange_kernel, cap, group),
        out_shape=(
            jax.ShapeDtypeStruct((LISTS, D), F32),
            jax.ShapeDtypeStruct((1, LISTS), F32),
        ),
        in_specs=[vmem, vmem],
        out_specs=(vmem, vmem),
        scratch_shapes=[
            pltpu.VMEM((PEERS * cap, VEC), BF),
            pltpu.VMEM((CHUNKS, PEERS * cap, WIDTH), BF),
            pltpu.VMEM((CHUNKS, PEERS * cap, WIDTH), BF),
            pltpu.VMEM((PEERS, 1, lanes), jnp.int32),
            pltpu.VMEM((PEERS, 1, lanes), jnp.int32),
            pltpu.VMEM((ZS, LISTS, PEERS * cap), BF),
            pltpu.VMEM((2, 4, 2, LISTS, WIDTH), F32),
            pltpu.VMEM((CHUNKS, 2, 2, 4, HALF, WIDTH), BF),
            pltpu.VMEM((CHUNKS, 2, 2, 4, HALF, WIDTH), BF),
            pltpu.VMEM((ZS, 1, LISTS), F32),
            pltpu.VMEM((ZS, 1, LISTS), F32),
            dma((CHUNKS,)), dma((CHUNKS,)), dma, dma,
            dma((CHUNKS,)), dma((CHUNKS, 2, 2, 4)),
            dma((ZS,)), dma((ZS,)),
        ],
        compiler_params=pltpu.CompilerParams(
            collective_id=number, has_side_effects=True, vmem_limit_bytes=63 * 2**20),
    )(err, plan)


def local(residuals, codes, list_ids, rotation, codebook, list_fill):
    err, plan, most = encode(residuals, codes.T, list_ids.reshape(1, VEC), rotation, codebook)
    sums, counts = lax.cond(
        most[0, 0] <= 64,
        functools.partial(exchange, 64, 2, 1),
        functools.partial(exchange, 96, 4, 2),
        err, plan)
    list_counts = counts.reshape(LISTS).astype(jnp.int32)
    divisor = jnp.maximum(list_counts, 1).astype(F32)
    list_drift = sums / divisor[:, None]
    new_blocks = (list_fill + list_counts + 127) // 128 - (list_fill + 127) // 128
    return list_drift, list_counts, new_blocks


def solution(mesh):
    split = P(("row", "col"))
    wide = P(("row", "col"), None)
    return jax.shard_map(
        local,
        mesh=mesh,
        in_specs=(wide, wide, split, P(), P(), split),
        out_specs=(wide, split, split),
        check_vma=False,
    )
```

```python
import functools

import jax
import jax.numpy as jnp
from jax import lax
from jax.experimental import pallas as pl
from jax.experimental.pallas import tpu as pltpu
from jax.sharding import PartitionSpec as P

MESH = pl.DeviceIdType.MESH
D = 768
M = 64
DSUB = 12
KSUB = 256
VEC = 1024
LISTS = 256
PEERS = 32
ZS = 8
CHUNKS = 6
WIDTH = D // CHUNKS
HALF = LISTS // 2
CAP = 64
REST = 32
F32 = jnp.float32
BF = jnp.bfloat16

_RING = (
    [(1, 2), (2, 1), (3, 2), (2, 3), (2, 2)]
    + [(1, 1), (3, 3), (1, 3), (3, 1)]
    + [(2, 0), (0, 2)]
    + [(1, 0), (0, 1), (3, 0), (0, 3)]
)
ORDER = [(a, b, 0) for a, b in _RING] + [(a, b, 1) for a, b in _RING] + [(0, 0, 1)]


def coords():
    row = lax.axis_index("row")
    col = lax.axis_index("col")
    return (row // 4) * 2 + col // 16, row % 4, (col // 2) % 8, col % 2


def device(x, y, z, c):
    return ((x // 2) * 4 + y, (x % 2) * 16 + z * 2 + c)


def greet(barrier, x, y, z, c):
    for dx, dy, dc in ORDER:
        pl.semaphore_signal(barrier, inc=1, device_id=device((x + dx) % 4, (y + dy) % 4, z, (c + dc) % 2), device_id_type=MESH)
    for dz in range(1, ZS):
        pl.semaphore_signal(barrier, inc=1, device_id=device(x, y, (z + dz) % 8, c), device_id_type=MESH)


def one_hot(names, index, start, size):
    shifted = index - start
    inside = jnp.logical_and(shifted >= 0, shifted < size)
    row = jnp.where(inside, shifted, -1).astype(F32).astype(BF)
    return jnp.where(names == row, jnp.ones((), BF), jnp.zeros((), BF))


def window_kernel(cap, group, base, res_hbm, codes_hbm, ids_ref, rot_hbm, book_hbm,
                  sums_ref, counts_ref, most_ref,
                  pair, weights, codes_ref, book_ref, table_ref, err, here_out, here_in, all_out, all_in,
                  pick, slots, rows, tag_out, tag_in, hot, part, z_out, z_in, cnt_out, cnt_in,
                  load_sem, here_ssem, here_rsem, all_ssem, all_rsem,
                  row_ssem, row_rsem, tag_ssem, tag_rsem, z_ssem, z_rsem, cnt_ssem, cnt_rsem):
    x, y, z, c = coords()
    me = (x * 4 + y) * 2 + c
    lanes = cap * group
    total_slots = PEERS * cap

    barrier = pltpu.get_barrier_semaphore()
    greet(barrier, x, y, z, c)
    loads = [
        pltpu.make_async_copy(src, dst, load_sem.at[i])
        for i, (src, dst) in enumerate([
            (book_hbm, book_ref), (codes_hbm, codes_ref),
            (res_hbm, pair.at[:, pl.ds(0, D)]), (rot_hbm, weights.at[pl.ds(0, D)])])
    ]
    for load in loads:
        load.start()

    ids = ids_ref[...]
    owner = ids // LISTS
    inner = ids % LISTS
    col = owner % 32
    row = owner // 32
    zed = (col // 2) % 8
    spot = (((row // 4) * 2 + col // 16) * 4 + row % 4) * 2 + col % 2
    at_peer = (lax.broadcasted_iota(jnp.int32, (PEERS, VEC), 0) == spot).astype(F32)
    blocks = jnp.concatenate([at_peer[:, b * 128:(b + 1) * 128] for b in range(VEC // 128)], axis=0).astype(BF)
    before = (lax.broadcasted_iota(jnp.int32, (128, 128), 0) < lax.broadcasted_iota(jnp.int32, (128, 128), 1)).astype(F32).astype(BF)
    inside = jnp.dot(blocks, before, preferred_element_type=F32)
    whole = jnp.dot(blocks, jnp.ones((128, 128), BF), preferred_element_type=F32)
    offset = jnp.zeros((PEERS, 128), F32)
    ranks = []
    for b in range(VEC // 128):
        ranks.append(jnp.sum((inside[b * PEERS:(b + 1) * PEERS] + offset) * at_peer[:, b * 128:(b + 1) * 128], axis=0, keepdims=True))
        offset = offset + whole[b * PEERS:(b + 1) * PEERS]
    rank = jnp.concatenate(ranks, axis=1).astype(jnp.int32) - base
    here_out[...] = jnp.max(offset, axis=0, keepdims=True)
    fits = jnp.logical_and(rank >= 0, rank < cap)
    slot = jnp.where(fits, spot * cap + rank, -1)
    lane = jnp.where(fits, rank + cap * (me % group), -1)

    wide_names = lax.broadcasted_iota(jnp.int32, (LISTS, VEC), 0).astype(F32).astype(BF)
    lane_hot = jnp.concatenate([one_hot(wide_names[:128], lane, j * 128, 128) for j in range(lanes // 128)], axis=0)
    tag_rows = jnp.concatenate([at_peer * (zed + 1).astype(F32), at_peer * inner.astype(F32)], axis=0).astype(BF)
    found = lax.dot_general(tag_rows, lane_hot, (((1,), (1,)), ((), ())), preferred_element_type=F32)
    tags = (found[:PEERS] - 1.0) * LISTS + found[PEERS:]
    tag_out[...] = tags.astype(jnp.int32).reshape(PEERS, 1, lanes)

    line = lax.broadcasted_iota(jnp.int32, (D, D), 0)
    feature = (line % M) * DSUB + line // M
    perm = (lax.broadcasted_iota(jnp.int32, (D, D), 1) == feature).astype(F32).astype(BF)
    weights[D:, :] = perm
    for load in loads[:2]:
        load.wait()
    table_ref[...] = -lax.dot_general(perm, book_ref[...], (((1,), (1,)), ((), ())), preferred_element_type=F32)
    for b in range(VEC // 128):
        index = codes_ref[:, b * 128:(b + 1) * 128]
        index = jnp.concatenate([index, index], axis=0)
        near = index % 128
        for j in range(D // 128):
            picked = jnp.where(
                index < 128,
                jnp.take_along_axis(table_ref[j * 128:(j + 1) * 128, :128], near, axis=1, mode="promise_in_bounds"),
                jnp.take_along_axis(table_ref[j * 128:(j + 1) * 128, 128:], near, axis=1, mode="promise_in_bounds"),
            )
            pair[b * 128:(b + 1) * 128, D + j * 128:D + (j + 1) * 128] = picked.T.astype(BF)
    for load in loads[2:]:
        load.wait()

    def encode(p):
        error = jnp.dot(pair[...], weights[:, 2 * p * WIDTH:2 * (p + 1) * WIDTH], preferred_element_type=F32).astype(BF)
        err[2 * p] = error[:, :WIDTH]
        err[2 * p + 1] = error[:, WIDTH:]

    def peer(o):
        dx, dy, dc = o
        px, py, pc = (x + dx) % 4, (y + dy) % 4, (c + dc) % 2
        return (px * 4 + py) * 2 + pc, device(px, py, z, pc)

    def tag_copy(k):
        spot, dev = peer(ORDER[k])
        return pltpu.make_async_remote_copy(
            tag_out.at[spot], tag_in.at[me], tag_ssem, tag_rsem, device_id=dev, device_id_type=MESH)

    def row_copy(ch, k):
        spot, dev = peer(ORDER[k])
        return pltpu.make_async_remote_copy(
            slots.at[ch, pl.ds(pl.multiple_of(spot * cap, 16), cap)],
            rows.at[ch, pl.ds(pl.multiple_of(me * cap, 16), cap)],
            row_ssem.at[ch], row_rsem.at[ch], device_id=dev, device_id_type=MESH)

    def own_copy(ch):
        span = pl.ds(pl.multiple_of(me * cap, 16), cap)
        return pltpu.make_async_copy(slots.at[ch, span], rows.at[ch, span], row_rsem.at[ch])

    def tag_keep():
        return pltpu.make_async_copy(tag_out.at[me], tag_in.at[me], tag_rsem)

    def place_first(i, _):
        start = pl.multiple_of(i * 256, 256)
        one = one_hot(wide_names, slot, start, 256)
        pick[pl.ds(start, 256), :] = one
        slots[0, pl.ds(start, 256), :] = jnp.dot(one, err[0], preferred_element_type=F32).astype(BF)
        return 0

    def place(ch):
        def one(i, _):
            start = pl.multiple_of(i * 512, 512)
            slots[ch, pl.ds(start, 512), :] = jnp.dot(
                pick[pl.ds(start, 512), :], err[ch], preferred_element_type=F32).astype(BF)
            return 0

        lax.fori_loop(0, total_slots // 512, one, 0)

    def send(ch):
        for k in range(len(ORDER)):
            row_copy(ch, k).start()
        own_copy(ch).start()

    encode(0)
    lax.fori_loop(0, total_slots // 256, place_first, 0)
    pl.semaphore_wait(barrier, len(ORDER) + ZS - 1)
    for k in range(len(ORDER)):
        tag_copy(k).start()
    tag_keep().start()
    send(0)
    for k in range(len(ORDER)):
        pltpu.make_async_remote_copy(
            here_out, here_in.at[k], here_ssem, here_rsem, device_id=peer(ORDER[k])[1], device_id_type=MESH).start()
    place(1)
    send(1)
    encode(1)
    encode(2)

    pltpu.make_async_copy(tag_in, tag_in, tag_rsem).wait()
    others = pl.ds(0, PEERS - 1)
    pltpu.make_async_copy(tag_out.at[others], tag_out.at[others], tag_ssem).wait()

    eye = (lax.broadcasted_iota(jnp.int32, (128, 128), 0) == lax.broadcasted_iota(jnp.int32, (128, 128), 1)).astype(F32)
    names = lax.broadcasted_iota(jnp.int32, (LISTS, 128), 0).astype(F32).astype(BF)
    tag = []
    for q in range(PEERS // group):
        joined = tag_in[q * group]
        for i in range(1, group):
            joined = jnp.maximum(joined, tag_in[q * group + i])
        tag += [joined[:, j * 128:(j + 1) * 128] for j in range(lanes // 128)]

    def make_hot(d, _):
        total = jnp.zeros((LISTS, 128), BF)
        for j in range(total_slots // 128):
            one = one_hot(names, tag[j], d * LISTS, LISTS)
            total = total + one
            hot[d, :, j * 128:(j + 1) * 128] = one
        spread = jnp.dot(total, jnp.ones((128, 128), BF), preferred_element_type=F32)
        for b in range(LISTS // 128):
            cnt_out[d, :, b * 128:(b + 1) * 128] = jnp.sum(spread[b * 128:(b + 1) * 128] * eye, axis=0, keepdims=True)
        return 0

    lax.fori_loop(0, ZS, make_hot, 0)

    def cnt_copy(dz):
        to = (z + dz) % 8
        return pltpu.make_async_remote_copy(
            cnt_out.at[to], cnt_in.at[z], cnt_ssem.at[dz], cnt_rsem.at[dz],
            device_id=device(x, y, to, c), device_id_type=MESH)

    pltpu.make_async_copy(here_in, here_in, here_rsem).wait()
    most = here_out[...]
    for k in range(len(ORDER)):
        most = jnp.maximum(most, here_in[k])
    all_out[...] = most
    for dz in range(1, ZS):
        cnt_copy(dz).start()
        pltpu.make_async_remote_copy(
            all_out, all_in.at[dz - 1], all_ssem, all_rsem,
            device_id=device(x, y, (z + dz) % 8, c), device_id_type=MESH).start()

    def length(h, s):
        return 4 if h == s else 3

    def z_copy(ch, h, s, t):
        to = (z + (1 if s == 0 else 7)) % 8
        return pltpu.make_async_remote_copy(
            z_out.at[ch, h, s, t], z_in.at[ch, h, s, t], z_ssem.at[ch], z_rsem.at[ch, h, s, t],
            device_id=device(x, y, to, c), device_id_type=MESH)

    def table(ch, d):
        return jnp.dot(hot[d], rows[ch], preferred_element_type=F32)

    def reduce(ch):
        pltpu.make_async_copy(rows.at[ch], rows.at[ch], row_rsem.at[ch]).wait()
        turn = ch % 3
        far = table(ch, (z + 4) % 8)
        for h in (0, 1):
            z_out[ch, h, h, 0] = far[h * HALF:(h + 1) * HALF].astype(BF)
            z_copy(ch, h, h, 0).start()
        for s in (0, 1):
            near = table(ch, (z + (3 if s == 0 else 5)) % 8)
            part[turn, 3, s] = near
            h = 1 - s
            z_out[ch, h, s, 0] = near[h * HALF:(h + 1) * HALF].astype(BF)
            z_copy(ch, h, s, 0).start()
        for k in (2, 1):
            for s in (0, 1):
                part[turn, k, s] = table(ch, (z + (k if s == 0 else 8 - k)) % 8)
        part[turn, 0, 0] = table(ch, z)

    def hop(ch, k):
        turn = ch % 3
        for h in (0, 1):
            for s in (0, 1):
                t = length(h, s) - k
                if t > 0:
                    z_copy(ch, h, s, t - 1).wait_recv()
                    own = part[turn, k, s, h * HALF:(h + 1) * HALF]
                    z_out[ch, h, s, t] = (own + z_in[ch, h, s, t - 1].astype(F32)).astype(BF)
                    z_copy(ch, h, s, t).start()

    def settle(ch):
        turn = ch % 3
        for h in (0, 1):
            total = part[turn, 0, 0, h * HALF:(h + 1) * HALF]
            for s in (0, 1):
                last = length(h, s) - 1
                z_copy(ch, h, s, last).wait_recv()
                total = total + z_in[ch, h, s, last].astype(F32)
            sums_ref[h * HALF:(h + 1) * HALF, pl.ds(pl.multiple_of(ch * WIDTH, WIDTH), WIDTH)] = total

    def period(ch, _):
        reduce(ch)

        @pl.when(ch > 1)
        def _():
            hop(ch - 2, 1)

        @pl.when(ch > 0)
        def _():
            hop(ch - 1, 2)

        @pl.when(ch + 2 < CHUNKS)
        def _():
            place(ch + 2)
            send(ch + 2)

        hop(ch, 3)

        @pl.when(ch > 1)
        def _():
            settle(ch - 2)

        return 0

    lax.fori_loop(0, CHUNKS, period, 0)
    hop(CHUNKS - 2, 1)
    hop(CHUNKS - 1, 2)
    settle(CHUNKS - 2)
    hop(CHUNKS - 1, 1)

    pltpu.make_async_copy(all_in, all_in, all_rsem).wait()
    for i in range(ZS - 1):
        most = jnp.maximum(most, all_in[i])
    most_ref[...] = most.astype(jnp.int32)
    total = cnt_out[z]
    for dz in range(1, ZS):
        cnt_copy(dz).wait()
        total = total + cnt_in[(z + 8 - dz) % 8]
    counts_ref[...] = total.astype(jnp.int32)
    pltpu.make_async_copy(here_in, here_in, here_ssem).wait()
    pltpu.make_async_copy(all_in, all_in, all_ssem).wait()

    def drain(ch, _):
        sent = slots.at[ch, pl.ds(0, (PEERS - 1) * cap)]
        pltpu.make_async_copy(sent, sent, row_ssem.at[ch]).wait()
        for piece in (z_out.at[ch, 0], z_out.at[ch, 1, pl.ds(0, 1)], z_out.at[ch, 1, 1, pl.ds(0, 2)]):
            pltpu.make_async_copy(piece, piece, z_ssem.at[ch]).wait()
        return 0

    lax.fori_loop(0, CHUNKS, drain, 0)
    settle(CHUNKS - 1)


def window(cap, group, base, number, residuals, codes, ids, rotation, codebook):
    vmem = pl.BlockSpec(memory_space=pltpu.VMEM)
    hbm = pl.BlockSpec(memory_space=pltpu.HBM)
    lanes = cap * group
    dma = pltpu.SemaphoreType.DMA
    return pl.pallas_call(
        functools.partial(window_kernel, cap, group, base),
        out_shape=(
            jax.ShapeDtypeStruct((LISTS, D), F32),
            jax.ShapeDtypeStruct((1, LISTS), jnp.int32),
            jax.ShapeDtypeStruct((1, 128), jnp.int32),
        ),
        in_specs=[hbm, hbm, vmem, hbm, hbm],
        out_specs=(vmem, vmem, vmem),
        scratch_shapes=[
            pltpu.VMEM((VEC, 2 * D), BF),
            pltpu.VMEM((2 * D, D), BF),
            pltpu.VMEM((M, VEC), jnp.int32),
            pltpu.VMEM((KSUB, D), BF),
            pltpu.VMEM((D, KSUB), F32),
            pltpu.VMEM((CHUNKS, VEC, WIDTH), BF),
            pltpu.VMEM((1, 128), F32),
            pltpu.VMEM((PEERS - 1, 1, 128), F32),
            pltpu.VMEM((1, 128), F32),
            pltpu.VMEM((ZS - 1, 1, 128), F32),
            pltpu.VMEM((PEERS * cap, VEC), BF),
            pltpu.VMEM((CHUNKS, PEERS * cap, WIDTH), BF),
            pltpu.VMEM((CHUNKS, PEERS * cap, WIDTH), BF),
            pltpu.VMEM((PEERS, 1, lanes), jnp.int32),
            pltpu.VMEM((PEERS, 1, lanes), jnp.int32),
            pltpu.VMEM((ZS, LISTS, PEERS * cap), BF),
            pltpu.VMEM((3, 4, 2, LISTS, WIDTH), F32),
            pltpu.VMEM((CHUNKS, 2, 2, 4, HALF, WIDTH), BF),
            pltpu.VMEM((CHUNKS, 2, 2, 4, HALF, WIDTH), BF),
            pltpu.VMEM((ZS, 1, LISTS), F32),
            pltpu.VMEM((ZS, 1, LISTS), F32),
            dma((4,)), dma, dma, dma, dma,
            dma((CHUNKS,)), dma((CHUNKS,)), dma, dma,
            dma((CHUNKS,)), dma((CHUNKS, 2, 2, 4)),
            dma((ZS,)), dma((ZS,)),
        ],
        compiler_params=pltpu.CompilerParams(
            collective_id=number, has_side_effects=True, vmem_limit_bytes=63 * 2**20),
    )(residuals, codes, ids, rotation, codebook)


def local(residuals, codes, list_ids, rotation, codebook, list_fill):
    given = (residuals, codes.T, list_ids.reshape(1, VEC), rotation, codebook)
    sums, counts, most = window(CAP, 2, 0, 0, *given)

    def rest(sums, counts, *given):
        more, extra, _ = window(REST, 4, CAP, 1, *given)
        return sums + more, counts + extra

    def done(sums, counts, *given):
        return sums, counts

    sums, counts = lax.cond(most[0, 0] > CAP, rest, done, sums, counts, *given)
    list_counts = counts.reshape(LISTS)
    divisor = jnp.maximum(list_counts, 1).astype(F32)
    list_drift = sums / divisor[:, None]
    new_blocks = (list_fill + list_counts + 127) // 128 - (list_fill + 127) // 128
    return list_drift, list_counts, new_blocks


def solution(mesh):
    split = P(("row", "col"))
    wide = P(("row", "col"), None)
    return jax.shard_map(
        local,
        mesh=mesh,
        in_specs=(wide, wide, split, P(), P(), split),
        out_specs=(wide, split, split),
        check_vma=False,
    )
```

```python
import functools

import jax
import jax.numpy as jnp
from jax import lax
from jax.experimental import pallas as pl
from jax.experimental.pallas import tpu as pltpu
from jax.sharding import PartitionSpec as P

MESH = pl.DeviceIdType.MESH
D = 768
M = 64
DSUB = 12
KSUB = 256
VEC = 1024
LISTS = 256
PEERS = 32
ZS = 8
CHUNKS = 6
WIDTH = D // CHUNKS
HALF = LISTS // 2
CAP = 64
REST = 32
F32 = jnp.float32
BF = jnp.bfloat16

_RING = (
    [(1, 2), (2, 1), (3, 2), (2, 3), (2, 2)]
    + [(1, 1), (3, 3), (1, 3), (3, 1)]
    + [(2, 0), (0, 2)]
    + [(1, 0), (0, 1), (3, 0), (0, 3)]
)
ORDER = [(a, b, 0) for a, b in _RING] + [(a, b, 1) for a, b in _RING] + [(0, 0, 1)]


def coords():
    row = lax.axis_index("row")
    col = lax.axis_index("col")
    return (row // 4) * 2 + col // 16, row % 4, (col // 2) % 8, col % 2


def device(x, y, z, c):
    return ((x // 2) * 4 + y, (x % 2) * 16 + z * 2 + c)


def greet(barrier, x, y, z, c):
    for dx, dy, dc in ORDER:
        pl.semaphore_signal(barrier, inc=1, device_id=device((x + dx) % 4, (y + dy) % 4, z, (c + dc) % 2), device_id_type=MESH)
    for dz in range(1, ZS):
        pl.semaphore_signal(barrier, inc=1, device_id=device(x, y, (z + dz) % 8, c), device_id_type=MESH)


def one_hot(names, index, start, size):
    shifted = index - start
    inside = jnp.logical_and(shifted >= 0, shifted < size)
    row = jnp.where(inside, shifted, -1).astype(F32).astype(BF)
    return jnp.where(names == row, jnp.ones((), BF), jnp.zeros((), BF))


def window_kernel(cap, group, base, res_hbm, codes_hbm, ids_ref, rot_hbm, book_hbm,
                  sums_ref, counts_ref, most_ref,
                  pair, weights, codes_ref, book_ref, table_ref, err, here_out, here_in, all_out, all_in,
                  pick, slots, rows, tag_out, tag_in, hot, part, z_out, z_in, cnt_out, cnt_in,
                  load_sem, here_ssem, here_rsem, all_ssem, all_rsem,
                  row_ssem, row_rsem, tag_ssem, tag_rsem, z_ssem, z_rsem, cnt_ssem, cnt_rsem):
    x, y, z, c = coords()
    me = (x * 4 + y) * 2 + c
    lanes = cap * group
    total_slots = PEERS * cap

    barrier = pltpu.get_barrier_semaphore()
    greet(barrier, x, y, z, c)
    loads = [
        pltpu.make_async_copy(src, dst, load_sem.at[i])
        for i, (src, dst) in enumerate([
            (book_hbm, book_ref), (codes_hbm, codes_ref),
            (res_hbm, pair.at[:, pl.ds(0, D)]), (rot_hbm, weights.at[pl.ds(0, D)])])
    ]
    for load in loads:
        load.start()

    ids = ids_ref[...]
    owner = ids // LISTS
    inner = ids % LISTS
    col = owner % 32
    row = owner // 32
    zed = (col // 2) % 8
    spot = (((row // 4) * 2 + col // 16) * 4 + row % 4) * 2 + col % 2
    at_peer = (lax.broadcasted_iota(jnp.int32, (PEERS, VEC), 0) == spot).astype(F32)
    blocks = jnp.concatenate([at_peer[:, b * 128:(b + 1) * 128] for b in range(VEC // 128)], axis=0).astype(BF)
    before = (lax.broadcasted_iota(jnp.int32, (128, 128), 0) < lax.broadcasted_iota(jnp.int32, (128, 128), 1)).astype(F32).astype(BF)
    inside = jnp.dot(blocks, before, preferred_element_type=F32)
    whole = jnp.dot(blocks, jnp.ones((128, 128), BF), preferred_element_type=F32)
    offset = jnp.zeros((PEERS, 128), F32)
    ranks = []
    for b in range(VEC // 128):
        ranks.append(jnp.sum((inside[b * PEERS:(b + 1) * PEERS] + offset) * at_peer[:, b * 128:(b + 1) * 128], axis=0, keepdims=True))
        offset = offset + whole[b * PEERS:(b + 1) * PEERS]
    rank = jnp.concatenate(ranks, axis=1).astype(jnp.int32) - base
    here_out[...] = jnp.max(offset, axis=0, keepdims=True)
    fits = jnp.logical_and(rank >= 0, rank < cap)
    slot = jnp.where(fits, spot * cap + rank, -1)
    lane = jnp.where(fits, rank + cap * (me % group), -1)

    wide_names = lax.broadcasted_iota(jnp.int32, (LISTS, VEC), 0).astype(F32).astype(BF)
    lane_hot = jnp.concatenate([one_hot(wide_names[:128], lane, j * 128, 128) for j in range(lanes // 128)], axis=0)
    tag_rows = jnp.concatenate([at_peer * (zed + 1).astype(F32), at_peer * inner.astype(F32)], axis=0).astype(BF)
    found = lax.dot_general(tag_rows, lane_hot, (((1,), (1,)), ((), ())), preferred_element_type=F32)
    tags = (found[:PEERS] - 1.0) * LISTS + found[PEERS:]
    tag_out[...] = tags.astype(jnp.int32).reshape(PEERS, 1, lanes)

    line = lax.broadcasted_iota(jnp.int32, (D, D), 0)
    feature = (line % M) * DSUB + line // M
    perm = (lax.broadcasted_iota(jnp.int32, (D, D), 1) == feature).astype(F32).astype(BF)
    weights[D:, :] = perm
    for load in loads[:2]:
        load.wait()
    table_ref[...] = -lax.dot_general(perm, book_ref[...], (((1,), (1,)), ((), ())), preferred_element_type=F32)
    for b in range(VEC // 128):
        index = codes_ref[:, b * 128:(b + 1) * 128]
        index = jnp.concatenate([index, index], axis=0)
        near = index % 128
        for j in range(D // 128):
            picked = jnp.where(
                index < 128,
                jnp.take_along_axis(table_ref[j * 128:(j + 1) * 128, :128], near, axis=1, mode="promise_in_bounds"),
                jnp.take_along_axis(table_ref[j * 128:(j + 1) * 128, 128:], near, axis=1, mode="promise_in_bounds"),
            )
            pair[b * 128:(b + 1) * 128, D + j * 128:D + (j + 1) * 128] = picked.T.astype(BF)
    for load in loads[2:]:
        load.wait()

    def encode(p):
        error = jnp.dot(pair[...], weights[:, 2 * p * WIDTH:2 * (p + 1) * WIDTH], preferred_element_type=F32).astype(BF)
        err[2 * p] = error[:, :WIDTH]
        err[2 * p + 1] = error[:, WIDTH:]

    def peer(o):
        dx, dy, dc = o
        px, py, pc = (x + dx) % 4, (y + dy) % 4, (c + dc) % 2
        return (px * 4 + py) * 2 + pc, device(px, py, z, pc)

    def tag_copy(k):
        spot, dev = peer(ORDER[k])
        return pltpu.make_async_remote_copy(
            tag_out.at[spot], tag_in.at[me], tag_ssem, tag_rsem, device_id=dev, device_id_type=MESH)

    def row_copy(ch, k):
        spot, dev = peer(ORDER[k])
        return pltpu.make_async_remote_copy(
            slots.at[ch, pl.ds(pl.multiple_of(spot * cap, 16), cap)],
            rows.at[ch, pl.ds(pl.multiple_of(me * cap, 16), cap)],
            row_ssem.at[ch], row_rsem.at[ch], device_id=dev, device_id_type=MESH)

    def own_copy(ch):
        span = pl.ds(pl.multiple_of(me * cap, 16), cap)
        return pltpu.make_async_copy(slots.at[ch, span], rows.at[ch, span], row_rsem.at[ch])

    def tag_keep():
        return pltpu.make_async_copy(tag_out.at[me], tag_in.at[me], tag_rsem)

    def place_first(i, _):
        start = pl.multiple_of(i * 256, 256)
        one = one_hot(wide_names, slot, start, 256)
        pick[pl.ds(start, 256), :] = one
        slots[0, pl.ds(start, 256), :] = jnp.dot(one, err[0], preferred_element_type=F32).astype(BF)
        return 0

    def place(ch):
        def one(i, _):
            start = pl.multiple_of(i * 512, 512)
            slots[ch, pl.ds(start, 512), :] = jnp.dot(
                pick[pl.ds(start, 512), :], err[ch], preferred_element_type=F32).astype(BF)
            return 0

        lax.fori_loop(0, total_slots // 512, one, 0)

    def send(ch):
        for k in range(len(ORDER)):
            row_copy(ch, k).start()
        own_copy(ch).start()

    pl.semaphore_wait(barrier, len(ORDER) + ZS - 1)
    for k in range(len(ORDER)):
        tag_copy(k).start()
    tag_keep().start()
    for k in range(len(ORDER)):
        pltpu.make_async_remote_copy(
            here_out, here_in.at[k], here_ssem, here_rsem, device_id=peer(ORDER[k])[1], device_id_type=MESH).start()
    encode(0)
    lax.fori_loop(0, total_slots // 256, place_first, 0)
    send(0)
    place(1)
    send(1)
    encode(1)
    encode(2)

    pltpu.make_async_copy(tag_in, tag_in, tag_rsem).wait()
    others = pl.ds(0, PEERS - 1)
    pltpu.make_async_copy(tag_out.at[others], tag_out.at[others], tag_ssem).wait()

    eye = (lax.broadcasted_iota(jnp.int32, (128, 128), 0) == lax.broadcasted_iota(jnp.int32, (128, 128), 1)).astype(F32)
    names = lax.broadcasted_iota(jnp.int32, (LISTS, 128), 0).astype(F32).astype(BF)
    tag = []
    for q in range(PEERS // group):
        joined = tag_in[q * group]
        for i in range(1, group):
            joined = jnp.maximum(joined, tag_in[q * group + i])
        tag += [joined[:, j * 128:(j + 1) * 128] for j in range(lanes // 128)]

    def make_hot(d, _):
        total = jnp.zeros((LISTS, 128), BF)
        for j in range(total_slots // 128):
            one = one_hot(names, tag[j], d * LISTS, LISTS)
            total = total + one
            hot[d, :, j * 128:(j + 1) * 128] = one
        spread = jnp.dot(total, jnp.ones((128, 128), BF), preferred_element_type=F32)
        for b in range(LISTS // 128):
            cnt_out[d, :, b * 128:(b + 1) * 128] = jnp.sum(spread[b * 128:(b + 1) * 128] * eye, axis=0, keepdims=True)
        return 0

    lax.fori_loop(0, ZS, make_hot, 0)

    def cnt_copy(dz):
        to = (z + dz) % 8
        return pltpu.make_async_remote_copy(
            cnt_out.at[to], cnt_in.at[z], cnt_ssem.at[dz], cnt_rsem.at[dz],
            device_id=device(x, y, to, c), device_id_type=MESH)

    pltpu.make_async_copy(here_in, here_in, here_rsem).wait()
    most = here_out[...]
    for k in range(len(ORDER)):
        most = jnp.maximum(most, here_in[k])
    all_out[...] = most
    for dz in range(1, ZS):
        cnt_copy(dz).start()
        pltpu.make_async_remote_copy(
            all_out, all_in.at[dz - 1], all_ssem, all_rsem,
            device_id=device(x, y, (z + dz) % 8, c), device_id_type=MESH).start()

    def length(h, s):
        return 4 if h == s else 3

    def z_copy(ch, h, s, t):
        to = (z + (1 if s == 0 else 7)) % 8
        return pltpu.make_async_remote_copy(
            z_out.at[ch, h, s, t], z_in.at[ch, h, s, t], z_ssem.at[ch], z_rsem.at[ch, h, s, t],
            device_id=device(x, y, to, c), device_id_type=MESH)

    def table(ch, d):
        return jnp.dot(hot[d], rows[ch], preferred_element_type=F32)

    def reduce(ch):
        pltpu.make_async_copy(rows.at[ch], rows.at[ch], row_rsem.at[ch]).wait()
        turn = ch % 5
        far = table(ch, (z + 4) % 8)
        for h in (0, 1):
            z_out[ch, h, h, 0] = far[h * HALF:(h + 1) * HALF].astype(BF)
            z_copy(ch, h, h, 0).start()
        for s in (0, 1):
            near = table(ch, (z + (3 if s == 0 else 5)) % 8)
            part[turn, 3, s] = near
            h = 1 - s
            z_out[ch, h, s, 0] = near[h * HALF:(h + 1) * HALF].astype(BF)
            z_copy(ch, h, s, 0).start()
        for k in (2, 1):
            for s in (0, 1):
                part[turn, k, s] = table(ch, (z + (k if s == 0 else 8 - k)) % 8)
        part[turn, 0, 0] = table(ch, z)

    def hop(ch, k):
        turn = ch % 5
        for h in (0, 1):
            for s in (0, 1):
                t = length(h, s) - k
                if t > 0:
                    z_copy(ch, h, s, t - 1).wait_recv()
                    own = part[turn, k, s, h * HALF:(h + 1) * HALF]
                    z_out[ch, h, s, t] = (own + z_in[ch, h, s, t - 1].astype(F32)).astype(BF)
                    z_copy(ch, h, s, t).start()

    def settle(ch):
        turn = ch % 5
        for h in (0, 1):
            total = part[turn, 0, 0, h * HALF:(h + 1) * HALF]
            for s in (0, 1):
                last = length(h, s) - 1
                z_copy(ch, h, s, last).wait_recv()
                total = total + z_in[ch, h, s, last].astype(F32)
            sums_ref[h * HALF:(h + 1) * HALF, pl.ds(pl.multiple_of(ch * WIDTH, WIDTH), WIDTH)] = total

    def count():
        total = cnt_out[z]
        for dz in range(1, ZS):
            cnt_copy(dz).wait()
            total = total + cnt_in[(z + 8 - dz) % 8]
        counts_ref[...] = total.astype(jnp.int32)
        pltpu.make_async_copy(all_in, all_in, all_rsem).wait()
        top = all_out[...]
        for i in range(ZS - 1):
            top = jnp.maximum(top, all_in[i])
        most_ref[...] = top.astype(jnp.int32)

    def period(ch, _):
        reduce(ch)

        @pl.when(ch >= 2)
        def _():
            hop(ch - 2, 1)

        @pl.when(ch >= 1)
        def _():
            hop(ch - 1, 2)

        @pl.when(ch >= 3)
        def _():
            settle(ch - 3)

        @pl.when(ch + 2 < CHUNKS)
        def _():
            place(ch + 2)
            send(ch + 2)

        @pl.when(ch == 1)
        def _():
            count()

        hop(ch, 3)
        return 0

    lax.fori_loop(0, CHUNKS, period, 0)
    hop(CHUNKS - 2, 1)
    hop(CHUNKS - 1, 2)
    settle(CHUNKS - 3)
    settle(CHUNKS - 2)
    hop(CHUNKS - 1, 1)

    pltpu.make_async_copy(here_in, here_in, here_ssem).wait()
    pltpu.make_async_copy(all_in, all_in, all_ssem).wait()

    def drain(ch, _):
        sent = slots.at[ch, pl.ds(0, (PEERS - 1) * cap)]
        pltpu.make_async_copy(sent, sent, row_ssem.at[ch]).wait()
        return 0

    lax.fori_loop(0, CHUNKS, drain, 0)
    settle(CHUNKS - 1)

    def drain_z(ch, _):
        for piece in (z_out.at[ch, 0], z_out.at[ch, 1, pl.ds(0, 1)], z_out.at[ch, 1, 1, pl.ds(0, 2)]):
            pltpu.make_async_copy(piece, piece, z_ssem.at[ch]).wait()
        return 0

    lax.fori_loop(0, CHUNKS, drain_z, 0)


def window(cap, group, base, number, residuals, codes, ids, rotation, codebook):
    vmem = pl.BlockSpec(memory_space=pltpu.VMEM)
    hbm = pl.BlockSpec(memory_space=pltpu.HBM)
    lanes = cap * group
    dma = pltpu.SemaphoreType.DMA
    return pl.pallas_call(
        functools.partial(window_kernel, cap, group, base),
        out_shape=(
            jax.ShapeDtypeStruct((LISTS, D), F32),
            jax.ShapeDtypeStruct((1, LISTS), jnp.int32),
            jax.ShapeDtypeStruct((1, 128), jnp.int32),
        ),
        in_specs=[hbm, hbm, vmem, hbm, hbm],
        out_specs=(vmem, vmem, vmem),
        scratch_shapes=[
            pltpu.VMEM((VEC, 2 * D), BF),
            pltpu.VMEM((2 * D, D), BF),
            pltpu.VMEM((M, VEC), jnp.int32),
            pltpu.VMEM((KSUB, D), BF),
            pltpu.VMEM((D, KSUB), F32),
            pltpu.VMEM((CHUNKS, VEC, WIDTH), BF),
            pltpu.VMEM((1, 128), F32),
            pltpu.VMEM((PEERS - 1, 1, 128), F32),
            pltpu.VMEM((1, 128), F32),
            pltpu.VMEM((ZS - 1, 1, 128), F32),
            pltpu.VMEM((PEERS * cap, VEC), BF),
            pltpu.VMEM((CHUNKS, PEERS * cap, WIDTH), BF),
            pltpu.VMEM((CHUNKS, PEERS * cap, WIDTH), BF),
            pltpu.VMEM((PEERS, 1, lanes), jnp.int32),
            pltpu.VMEM((PEERS, 1, lanes), jnp.int32),
            pltpu.VMEM((ZS, LISTS, PEERS * cap), BF),
            pltpu.VMEM((5, 4, 2, LISTS, WIDTH), F32),
            pltpu.VMEM((CHUNKS, 2, 2, 4, HALF, WIDTH), BF),
            pltpu.VMEM((CHUNKS, 2, 2, 4, HALF, WIDTH), BF),
            pltpu.VMEM((ZS, 1, LISTS), F32),
            pltpu.VMEM((ZS, 1, LISTS), F32),
            dma((4,)), dma, dma, dma, dma,
            dma((CHUNKS,)), dma((CHUNKS,)), dma, dma,
            dma((CHUNKS,)), dma((CHUNKS, 2, 2, 4)),
            dma((ZS,)), dma((ZS,)),
        ],
        compiler_params=pltpu.CompilerParams(
            collective_id=number, has_side_effects=True, vmem_limit_bytes=63 * 2**20),
    )(residuals, codes, ids, rotation, codebook)


def local(residuals, codes, list_ids, rotation, codebook, list_fill):
    given = (residuals, codes.T, list_ids.reshape(1, VEC), rotation, codebook)
    sums, counts, most = window(CAP, 2, 0, 0, *given)

    def rest(sums, counts, *given):
        more, extra, _ = window(REST, 4, CAP, 1, *given)
        return sums + more, counts + extra

    def done(sums, counts, *given):
        return sums, counts

    sums, counts = lax.cond(most[0, 0] > CAP, rest, done, sums, counts, *given)
    list_counts = counts.reshape(LISTS)
    divisor = jnp.maximum(list_counts, 1).astype(F32)
    list_drift = sums / divisor[:, None]
    new_blocks = (list_fill + list_counts + 127) // 128 - (list_fill + 127) // 128
    return list_drift, list_counts, new_blocks


def solution(mesh):
    split = P(("row", "col"))
    wide = P(("row", "col"), None)
    return jax.shard_map(
        local,
        mesh=mesh,
        in_specs=(wide, wide, split, P(), P(), split),
        out_specs=(wide, split, split),
        check_vma=False,
    )
```
